512 devices in a mesh: sec: 16 (over z_hi, y, core), gx: 32 (over x, z_lo).
Axes of the slice: x: 4, y: 4, z: 16 (z_hi: 2, z_lo: 8; z = z_hi * 8 + z_lo), core: 2. Of those that a mesh axis runs over, the one named last changes fastest.
Arguments:
- incoming: float32 [16, 128, 64, 256], P('sec', 'gx'), may hold values from 0.5 to 2
- backward: bfloat16 [64, 128, 64, 256], P('sec', 'gx'), may hold values from 0.5 to 2
- fields: float32 [3, 128, 256], P(None, 'gx'), may hold values from -0.4 to 0.4
- block_types: int32 [16, 4], P('sec'), may hold values from 0 to 2
- axial_taps: float32 [3, 64], replicated, may hold values from 0.1 to 0.45
- lateral_taps: float32 [3, 64], replicated, may hold values from 0.1 to 0.45
- depth_taps: float32 [3, 64], replicated, may hold values from 0.1 to 0.45
- bend_diagonal: float32 [64], replicated, may hold values from 0.4 to 0.8
- bend_coupling: float32 [64, 64], replicated, may hold values from 0 to 0.025
Outputs:
- handoff: float32 [16, 128, 64, 256], P('sec', 'gx')
- density: float32 [128, 64, 256], P('gx', 'sec')
The draws below stay inside these ranges and needn't reach their ends.
All inputs are finite; a program needn't handle non-finite values.
Results may differ from the reference program's by a relative error of at most 0.0003.
Values sent between devices are 32-bit elements; how exact they have to be, the bound alone decides.
A program may use at most 64 MiB of HBM per device.

```python
import math
import jax
import jax.numpy as jnp
from jax import lax

ORIENT = 64
NTYPES = 3
STEPS = 4
TICKS = 3
NX = 128
NY = 4
NZ = 64
CONTOUR = 64
N_SEC = 16


def touch_ends(drawn, own_key, least, largest):
    spot = [jax.random.randint(jax.random.fold_in(own_key, axis), (), 0, length) for axis, length in enumerate(drawn.shape)]
    longest = drawn.shape.index(max(drawn.shape))
    neighbour = spot[:longest] + [(spot[longest] + 1) % drawn.shape[longest]] + spot[longest + 1:]
    return drawn.at[tuple(spot)].set(least).at[tuple(neighbour)].set(largest)


def block_scale(key, dims, pieces, least, largest):
    loudness = 1.0
    for dim, blocks in pieces:
        heights = jax.random.uniform(jax.random.fold_in(jax.random.fold_in(key, 6), dim), (blocks,), jnp.float32, least / len(pieces), largest / len(pieces))
        loudness = loudness * jnp.repeat(jnp.exp(heights), dims[dim] // blocks).reshape((-1,) + (1,) * (len(dims) - 1 - dim))
    return loudness


def setup_inputs(seed: int = 0) -> dict:
    seeds = jax.random.split(jax.random.key(seed), 10)
    return {
        "incoming": jnp.clip(jnp.exp(math.log(2.0) - 1.3862944 * jax.random.uniform(seeds[0], (N_SEC, NX, ORIENT, NY * NZ), jnp.float32) ** block_scale(seeds[0], (N_SEC, NX, ORIENT, NY * NZ), ((0, 16), (1, 32)), -0.2, 0.2)), 0.5, 2.0),
        "backward": jnp.clip(jnp.exp(math.log(2.0) - 1.3862944 * jax.random.uniform(seeds[1], (CONTOUR, NX, ORIENT, NY * NZ), jnp.float32) ** block_scale(seeds[1], (CONTOUR, NX, ORIENT, NY * NZ), ((0, 16), (1, 32)), -0.2, 0.2)), 0.5, 2.0).astype(jnp.bfloat16),
        "fields": jnp.clip(jax.random.uniform(seeds[2], (NTYPES, NX, NY * NZ), jnp.float32, -0.4, 0.4) * block_scale(seeds[2], (NTYPES, NX, NY * NZ), ((1, 32),), -0.4, 0.0), -0.4, 0.4),
        "block_types": touch_ends(jax.random.randint(seeds[3], (N_SEC, STEPS), 0, NTYPES), jax.random.fold_in(seeds[3], 1), 0, NTYPES - 1).astype(jnp.int32),
        "axial_taps": jnp.clip(jax.random.uniform(seeds[4], (3, ORIENT), jnp.float32, 0.1, 0.45), 0.1, 0.45),
        "lateral_taps": jnp.clip(jax.random.uniform(seeds[5], (3, ORIENT), jnp.float32, 0.1, 0.45), 0.1, 0.45),
        "depth_taps": jnp.clip(jax.random.uniform(seeds[6], (3, ORIENT), jnp.float32, 0.1, 0.45), 0.1, 0.45),
        "bend_diagonal": jnp.clip(jax.random.uniform(seeds[7], (ORIENT,), jnp.float32, 0.4, 0.8), 0.4, 0.8),
        "bend_coupling": jnp.clip(jax.random.uniform(seeds[8], (ORIENT, ORIENT), jnp.float32, 0.0, 0.025), 0.0, 0.025),
    }


def boltzmann(fields, kinds):
    selector = kinds == jnp.arange(fields.shape[0], dtype=jnp.int32)
    chosen = jnp.sum(jnp.where(selector[:, None, None], fields, jnp.zeros_like(fields)), axis=0)
    return jnp.exp(-chosen)


def column(taps, which):
    return taps[which][None, :, None, None]


def advance(propagator, factor, axial_taps, lateral_taps, depth_taps, kernel):
    planes = propagator.shape[0]
    orients = propagator.shape[1]
    cube = propagator.reshape(planes, orients, NY, NZ)
    along_x = column(axial_taps, 0) * jnp.roll(cube, 1, axis=0) + column(axial_taps, 1) * cube + column(axial_taps, 2) * jnp.roll(cube, -1, axis=0)
    along_y = column(lateral_taps, 0) * jnp.roll(along_x, 1, axis=2) + column(lateral_taps, 1) * along_x + column(lateral_taps, 2) * jnp.roll(along_x, -1, axis=2)
    along_z = column(depth_taps, 0) * jnp.roll(along_y, 1, axis=3) + column(depth_taps, 1) * along_y + column(depth_taps, 2) * jnp.roll(along_y, -1, axis=3)
    blended = jnp.einsum("uv,xvyz->xuyz", kernel, along_z, precision=lax.Precision.HIGHEST)
    return blended.reshape(propagator.shape) * factor[:, None, :]


def reference(incoming, backward, fields, block_types, axial_taps, lateral_taps, depth_taps, bend_diagonal, bend_coupling):
    kernel = jnp.diag(bend_diagonal) + bend_coupling
    steps_each = block_types.shape[1]
    stored_all = backward.reshape((N_SEC, steps_each) + backward.shape[1:])

    def section(density_part, items):
        propagator, kinds, stored = items
        for position in range(steps_each):
            factor = boltzmann(fields, kinds[position])
            propagator = advance(propagator, factor, axial_taps, lateral_taps, depth_taps, kernel)
            density_part = density_part + propagator * stored[position].astype(jnp.float32)
        return density_part, propagator

    current = incoming
    density_sum = jnp.zeros(incoming.shape[1:], jnp.float32)
    outgoing = incoming
    for tick_index in range(TICKS):
        density_sum, outgoing = lax.scan(section, jnp.zeros(incoming.shape[1:], jnp.float32), (current, block_types, stored_all))
        if tick_index + 1 < TICKS:
            current = jnp.concatenate([incoming[:1], outgoing[:-1]], axis=0)
    density = density_sum / (N_SEC * steps_each)
    return outgoing, density
```

```python
import functools

import jax
import jax.numpy as jnp
from jax import lax
from jax.experimental import pallas as pl
from jax.experimental.pallas import tpu as pltpu
from jax.sharding import PartitionSpec as P

MESH = pl.DeviceIdType.MESH
PLANES = 4
LEVELS = 12
SPAN = PLANES + 2 * LEVELS
OWN = LEVELS
ORIENT = 64
CELLS = 256


def body(
    n_gx, contour,
    inc, back, fld, btr, taps, kmat,
    hand, den,
    lev, fw, bt, part, summed, kcat, r_core, r_y, s_y, r_z,
    mv_send, mv_recv, mv_extra, h_send, h_recv, f_send, f_recv, b_send, b_recv,
    loc, c_send, c_recv, y_send, y_recv, z_send, z_recv,
):
    k = lax.axis_index("sec")
    g = lax.axis_index("gx")
    core = lax.rem(k, 2)
    y = lax.rem(lax.div(k, 2), 4)
    zhi = lax.div(k, 8)
    right = lax.rem(g + 1, n_gx)
    left = lax.rem(g + n_gx - 1, n_gx)
    other_core = k + 1 - 2 * core
    other_z = lax.rem(k + 8, 16)

    def across(dy):
        return 8 * zhi + 2 * lax.rem(y + dy, 4) + core

    bt[pl.ds(0, 8)] = jnp.zeros((8, 1, CELLS), jnp.float32)
    barrier = pltpu.get_barrier_semaphore()
    sections = [lax.rem(k + n, 16) for n in (1, 2, 14, 15)]
    sections += [other_core, other_z] + [across(n) for n in (1, 2, 3)]
    for n in sections:
        pl.semaphore_signal(barrier, inc=1, device_id=(n, g), device_id_type=MESH)
    for n in (left, right):
        pl.semaphore_signal(barrier, inc=1, device_id=(k, n), device_id_type=MESH)

    own_fw = pltpu.make_async_copy(fld, fw.at[pl.ds(OWN, PLANES)], loc.at[0])
    own_bt = pltpu.make_async_copy(btr, bt.at[pl.ds(8, 4)], loc.at[1])
    own_fw.start()
    own_bt.start()
    full = kmat[...]
    high = full.astype(jnp.bfloat16)
    low = (full - high.astype(jnp.float32)).astype(jnp.bfloat16)
    col = lax.broadcasted_iota(jnp.int32, full.shape, 1)
    mixed = jnp.where(
        jnp.logical_and(col >= ORIENT, col < 2 * ORIENT), low.astype(jnp.float32), high.astype(jnp.float32)
    )
    kcat[...] = mixed.astype(jnp.bfloat16)
    own_fw.wait()
    own_bt.wait()

    pl.semaphore_wait(barrier, 11)

    def move(p, target, send, recv):
        return pltpu.make_async_remote_copy(
            src_ref=inc.at[p], dst_ref=lev.at[OWN + p], send_sem=send, recv_sem=recv,
            device_id=(target, g), device_id_type=MESH,
        )

    def halo_right(d):
        return pltpu.make_async_remote_copy(
            src_ref=lev.at[OWN + PLANES - d], dst_ref=lev.at[OWN - d],
            send_sem=h_send.at[0, d - 1], recv_sem=h_recv.at[0, d - 1],
            device_id=(k, right), device_id_type=MESH,
        )

    def halo_left(d):
        return pltpu.make_async_remote_copy(
            src_ref=lev.at[OWN - 1 + d], dst_ref=lev.at[OWN + PLANES - 1 + d],
            send_sem=h_send.at[1, d - 1], recv_sem=h_recv.at[1, d - 1],
            device_id=(k, left), device_id_type=MESH,
        )

    def field_right(r):
        return pltpu.make_async_remote_copy(
            src_ref=fw.at[pl.ds(OWN + PLANES - PLANES * r, PLANES)],
            dst_ref=fw.at[pl.ds(OWN - PLANES * r, PLANES)],
            send_sem=f_send.at[0, r - 1], recv_sem=f_recv.at[0, r - 1],
            device_id=(k, right), device_id_type=MESH,
        )

    def field_left(r):
        return pltpu.make_async_remote_copy(
            src_ref=fw.at[pl.ds(OWN - PLANES + PLANES * r, PLANES)],
            dst_ref=fw.at[pl.ds(OWN + PLANES * r, PLANES)],
            send_sem=f_send.at[1, r - 1], recv_sem=f_recv.at[1, r - 1],
            device_id=(k, left), device_id_type=MESH,
        )

    def kinds(ahead):
        return pltpu.make_async_remote_copy(
            src_ref=btr, dst_ref=bt.at[pl.ds(8 - 4 * ahead, 4)],
            send_sem=b_send.at[ahead - 1], recv_sem=b_recv.at[ahead - 1],
            device_id=(lax.rem(k + ahead, 16), g), device_id_type=MESH,
        )

    order = (3, 0, 2, 1)

    @pl.when(k <= 13)
    def _():
        for p in order:
            move(p, lax.rem(k + 2, 16), mv_send.at[p], mv_recv.at[p]).start()
        kinds(2).start()

    @pl.when(k <= 14)
    def _():
        kinds(1).start()

    @pl.when(k == 0)
    def _():
        for p in order:
            move(p, 1, mv_extra.at[p], mv_recv.at[p]).start()
        for p in order:
            pltpu.make_async_copy(inc.at[p], lev.at[OWN + p], mv_recv.at[p]).start()

    field_right(1).start()
    field_left(1).start()

    def arrive(p):
        @pl.when(k == 0)
        def _():
            pltpu.make_async_copy(inc.at[p], lev.at[OWN + p], mv_recv.at[p]).wait()

        @pl.when(k > 0)
        def _():
            move(p, lax.rem(k + 2, 16), mv_send.at[p], mv_recv.at[p]).wait_recv()

    arrive(3)
    halo_right(1).start()
    arrive(0)
    halo_left(1).start()
    arrive(2)
    halo_right(2).start()
    arrive(1)
    halo_left(2).start()
    halo_right(3).start()
    halo_left(3).start()
    halo_right(4).start()
    halo_left(4).start()

    @pl.when(k >= 1)
    def _():
        kinds(1).wait_recv()

    @pl.when(k >= 2)
    def _():
        kinds(2).wait_recv()

    lane = lax.broadcasted_iota(jnp.int32, (ORIENT, 128), 1)
    in_low = lane < 64
    at_first = lax.rem(lane, 64) == 0
    at_last = lax.rem(lane, 64) == 63

    def blend(p, src, kinds_row):
        ax0, ax2, la0, la2, de0, de2 = [taps[n] for n in range(6)]
        halves = []
        for h in range(2):
            lanes = pl.ds(128 * h, 128)
            halves.append(
                ax0 * lev[src + p - 1, :, lanes] + lev[src + p, :, lanes] + ax2 * lev[src + p + 1, :, lanes]
            )
        a0, a1 = halves
        r0 = pltpu.roll(a0, 64, 1)
        r1 = pltpu.roll(a1, 64, 1)
        near = jnp.where(in_low, r1, r0)
        far = jnp.where(in_low, r0, r1)
        b0 = la0 * near + a0 + la2 * far
        b1 = la0 * far + a1 + la2 * near
        es = []
        for b in (b0, b1):
            turned = pltpu.roll(b, 64, 1)
            behind = pltpu.roll(jnp.where(at_last, turned, b), 1, 1)
            ahead = pltpu.roll(jnp.where(at_first, turned, b), 127, 1)
            es.append(de0 * behind + b + de2 * ahead)
        e = jnp.concatenate(es, axis=1)
        e_high = e.astype(jnp.bfloat16)
        e_low = (e - e_high.astype(jnp.float32)).astype(jnp.bfloat16)
        stacked = jnp.concatenate([e_high, e_high, e_low], axis=0)
        c = jnp.dot(kcat[...], stacked, preferred_element_type=jnp.float32)
        chosen = jnp.where(kinds_row == 0.0, fw[p, 0], jnp.where(kinds_row == 1.0, fw[p, 1], fw[p, 2]))
        return c * jnp.exp(-chosen)

    def stage_steps(d, s, carry):
        row = bt[s - 1]
        restart0 = jnp.logical_and(k == 0, s == 9)
        restart1 = jnp.logical_and(k == 1, s == 5)
        level = jnp.where(jnp.logical_or(restart0, restart1), 0, s - 1)
        src = level * SPAN
        p_left = OWN - d + s
        p_right = OWN + PLANES - 1 + d - s
        new_left = blend(p_left, src, row)
        new_right = blend(p_right, src, row)
        lev[s * SPAN + p_left] = new_left
        lev[s * SPAN + p_right] = new_right
        return carry

    stage_steps(0, 1, 0)

    def stage(d, carry):
        halo_right(d).wait_recv()

        @pl.when(d <= LEVELS - PLANES)
        def _():
            halo_right(d + PLANES).start()

        halo_left(d).wait_recv()

        @pl.when(d <= LEVELS - PLANES)
        def _():
            halo_left(d + PLANES).start()

        @pl.when(lax.rem(d, 4) == 1)
        def _():
            r = lax.div(d + 3, 4)
            field_right(r).wait_recv()
            field_left(r).wait_recv()

            @pl.when(r < 3)
            def _():
                field_right(r + 1).start()
                field_left(r + 1).start()

        lax.fori_loop(1, jnp.minimum(d + 1, LEVELS) + 1, functools.partial(stage_steps, d), 0)
        return carry

    lax.fori_loop(1, LEVELS + 1, stage, 0)

    for p in range(PLANES):
        hand[p] = lev[LEVELS * SPAN + OWN + p]
        for n in range(8):
            rows = pl.ds(8 * n, 8)
            total = jnp.zeros((8, CELLS), jnp.float32)
            for j in range(4):
                total += lev[(9 + j) * SPAN + OWN + p, rows] * back[j, p, rows].astype(jnp.float32)
            part[0, n % 4, n // 4, p] = total[:4]
            part[1, n % 4, n // 4, p] = total[4:]

    to_core = pltpu.make_async_remote_copy(
        src_ref=part.at[1 - core], dst_ref=r_core, send_sem=c_send, recv_sem=c_recv,
        device_id=(other_core, g), device_id_type=MESH,
    )
    to_core.start()
    to_core.wait_recv()
    summed[...] = part[core] + r_core[...]

    def to_y(dy):
        return pltpu.make_async_remote_copy(
            src_ref=summed.at[lax.rem(y + dy, 4)], dst_ref=r_y.at[dy - 1],
            send_sem=y_send.at[dy - 1], recv_sem=y_recv.at[dy - 1],
            device_id=(across(dy), g), device_id_type=MESH,
        )

    for dy in (2, 1, 3):
        to_y(dy).start()
    for dy in (1, 3, 2):
        to_y(dy).wait_recv()
    s_y[...] = summed[y] + r_y[0] + r_y[1] + r_y[2]
    to_z = pltpu.make_async_remote_copy(
        src_ref=s_y.at[1 - zhi], dst_ref=r_z, send_sem=z_send, recv_sem=z_recv,
        device_id=(other_z, g), device_id_type=MESH,
    )
    to_z.start()

    def drain(d, carry):
        halo_right(d).wait_send()
        halo_left(d).wait_send()
        return carry

    lax.fori_loop(1, LEVELS + 1, drain, 0)
    for r in (1, 2, 3):
        field_right(r).wait_send()
        field_left(r).wait_send()

    @pl.when(k <= 13)
    def _():
        for p in order:
            move(p, lax.rem(k + 2, 16), mv_send.at[p], mv_recv.at[p]).wait_send()
        kinds(2).wait_send()

    @pl.when(k <= 14)
    def _():
        kinds(1).wait_send()

    @pl.when(k == 0)
    def _():
        for p in order:
            move(p, 1, mv_extra.at[p], mv_recv.at[p]).wait_send()

    to_core.wait_send()
    for dy in (1, 2, 3):
        to_y(dy).wait_send()
    to_z.wait()
    den[...] = (s_y[zhi] + r_z[...]) / contour


def per_device(
    incoming, backward, fields, block_types,
    axial_taps, lateral_taps, depth_taps, bend_diagonal, bend_coupling,
):
    n_gx = lax.axis_size("gx")
    contour = float(lax.axis_size("sec") * block_types.shape[1])
    ratios = jnp.stack(
        [t[n] / t[1] for t in (axial_taps, lateral_taps, depth_taps) for n in (0, 2)]
    )
    taps = jnp.broadcast_to(ratios[:, :, None], (6, ORIENT, 128))
    kernel = jnp.diag(bend_diagonal) + bend_coupling
    kernel = kernel * (axial_taps[1] * lateral_taps[1] * depth_taps[1])[None, :]
    kmat = jnp.concatenate([kernel, kernel, kernel], axis=1)
    fld = jnp.transpose(fields, (1, 0, 2))[:, :, None, :]
    btr = jnp.broadcast_to(block_types[0].astype(jnp.float32)[:, None, None], (4, 1, CELLS))
    vmem = pl.BlockSpec(memory_space=pltpu.VMEM)
    dma = pltpu.SemaphoreType.DMA
    f32 = jnp.float32
    hand, den = pl.pallas_call(
        functools.partial(body, n_gx, contour),
        out_shape=(
            jax.ShapeDtypeStruct((PLANES, ORIENT, CELLS), f32),
            jax.ShapeDtypeStruct((PLANES, 4, CELLS), f32),
        ),
        in_specs=[vmem] * 6,
        out_specs=(vmem, vmem),
        scratch_shapes=[
            pltpu.VMEM(((LEVELS + 1) * SPAN, ORIENT, CELLS), f32),
            pltpu.VMEM((SPAN, 3, 1, CELLS), f32),
            pltpu.VMEM((LEVELS, 1, CELLS), f32),
            pltpu.VMEM((2, 4, 2, PLANES, 4, CELLS), f32),
            pltpu.VMEM((4, 2, PLANES, 4, CELLS), f32),
            pltpu.VMEM((ORIENT, 3 * ORIENT), jnp.bfloat16),
            pltpu.VMEM((4, 2, PLANES, 4, CELLS), f32),
            pltpu.VMEM((3, 2, PLANES, 4, CELLS), f32),
            pltpu.VMEM((2, PLANES, 4, CELLS), f32),
            pltpu.VMEM((PLANES, 4, CELLS), f32),
            dma((4,)), dma((4,)), dma((4,)),
            dma((2, LEVELS)), dma((2, LEVELS)),
            dma((2, 3)), dma((2, 3)),
            dma((2,)), dma((2,)),
            dma((2,)),
            dma(()), dma(()),
            dma((3,)), dma((3,)),
            dma(()), dma(()),
        ],
        compiler_params=pltpu.CompilerParams(
            collective_id=0, has_side_effects=True, vmem_limit_bytes=48 << 20
        ),
        name="chain",
    )(incoming[0], backward, fld, btr, taps, kmat)
    return hand[None], den


def solution(mesh):
    in_specs = (
        P("sec", "gx", None, None),
        P("sec", "gx", None, None),
        P(None, "gx", None),
        P("sec", None),
        P(), P(), P(), P(), P(),
    )
    out_specs = (P("sec", "gx", None, None), P("gx", "sec", None))
    return jax.shard_map(
        per_device, mesh=mesh, in_specs=in_specs, out_specs=out_specs, check_vma=False
    )
```

```python
import functools

import jax
import jax.numpy as jnp
from jax import lax
from jax.experimental import pallas as pl
from jax.experimental.pallas import tpu as pltpu
from jax.sharding import PartitionSpec as P

MESH = pl.DeviceIdType.MESH
PLANES = 4
LEVELS = 12
SPAN = PLANES + 2 * LEVELS
OWN = LEVELS
ORIENT = 64
CELLS = 256
SLOTS = 15


def body(
    n_gx, contour,
    inc, back, fld, btr, taps, weights,
    hand, den,
    lev, q, pad, fw, factors, bt, pick, back_t, wcat, part, summed, relay, r_core, r_y, s_y, r_z,
    mv_send, mv_recv, mv_extra, relay_sem, h_send, h_recv, f_send, f_recv, b_send, b_recv,
    loc, c_send, c_recv, y_send, y_recv, z_send, z_recv,
):
    k = lax.axis_index("sec")
    g = lax.axis_index("gx")
    core = lax.rem(k, 2)
    y = lax.rem(lax.div(k, 2), 4)
    zhi = lax.div(k, 8)
    right = lax.rem(g + 1, n_gx)
    left = lax.rem(g + n_gx - 1, n_gx)
    other_core = k + 1 - 2 * core
    other_z = lax.rem(k + 8, 16)
    relays = k < 6
    crosses = jnp.logical_and(k >= 6, k <= 7)

    def across(dy):
        return 8 * zhi + 2 * lax.rem(y + dy, 4) + core

    bt[pl.ds(0, 8)] = jnp.zeros((8, 1, 128), jnp.float32)
    barrier = pltpu.get_barrier_semaphore()
    sections = [lax.rem(k + n, 16) for n in (1, 2, 14, 15)]
    sections += [other_core, other_z] + [across(n) for n in (1, 2, 3)]
    for n in sections:
        pl.semaphore_signal(barrier, inc=1, device_id=(n, g), device_id_type=MESH)
    for n in (left, right):
        pl.semaphore_signal(barrier, inc=1, device_id=(k, n), device_id_type=MESH)

    @pl.when(jnp.logical_and(k >= 8, k <= 9))
    def _():
        for n in (4, 6):
            pl.semaphore_signal(barrier, inc=1, device_id=(k - n, g), device_id_type=MESH)

    own_fw = pltpu.make_async_copy(fld, fw.at[3], loc.at[0])
    own_bt = pltpu.make_async_copy(btr, bt.at[pl.ds(8, 4)], loc.at[1])
    own_fw.start()
    own_bt.start()
    full = weights[...]
    high = full.astype(jnp.bfloat16)
    low = (full - high.astype(jnp.float32)).astype(jnp.bfloat16)
    for n in range(2):
        wcat[pl.ds(128 * n, 128), pl.ds(0, 128)] = high
        wcat[pl.ds(128 * n, 128), pl.ds(128, 128)] = low
    for j in range(4):
        for n, (p_left, p_right) in enumerate(((1, 2), (0, 3))):
            both = jnp.concatenate([back[j, p_left], back[j, p_right]], axis=0)
            back_t[j, n] = jnp.transpose(both.astype(jnp.float32))
    own_fw.wait()
    own_bt.wait()

    def pair_factor(j, slab_left, row_left, slab_right, row_right):
        rows = []
        for t in range(3):
            rows.append(jnp.exp(-fw[slab_left, t, pl.ds(row_left, 1)]))
            rows.append(jnp.exp(-fw[slab_right, t, pl.ds(row_right, 1)]))
        rows = jnp.concatenate(rows + [jnp.zeros((2, CELLS), jnp.float32)], axis=0)
        first = rows.astype(jnp.bfloat16).astype(jnp.float32)
        rest = rows - first
        second = rest.astype(jnp.bfloat16).astype(jnp.float32)
        stack = [first, second, rest - second, jnp.zeros((104, CELLS), jnp.float32)]
        factors[j] = jnp.transpose(jnp.concatenate(stack, axis=0)).astype(jnp.bfloat16)

    pair_factor(0, 3, 1, 3, 2)
    pair_factor(1, 3, 0, 3, 3)

    @pl.when(jnp.logical_and(k >= 2, k <= 5))
    def _():
        pl.semaphore_wait(barrier, 12)

    @pl.when(jnp.logical_or(k < 2, k > 5))
    def _():
        pl.semaphore_wait(barrier, 11)

    def move(p, target, send, recv):
        return pltpu.make_async_remote_copy(
            src_ref=inc.at[p], dst_ref=lev.at[OWN + p], send_sem=send, recv_sem=recv,
            device_id=(target, g), device_id_type=MESH,
        )

    def to_relay(p):
        return pltpu.make_async_remote_copy(
            src_ref=inc.at[p], dst_ref=relay, send_sem=mv_send.at[p], recv_sem=relay_sem.at[0],
            device_id=(2 * p + core, g), device_id_type=MESH,
        )

    def from_relay():
        return pltpu.make_async_remote_copy(
            src_ref=relay, dst_ref=lev.at[OWN + y], send_sem=relay_sem.at[1], recv_sem=mv_recv.at[y],
            device_id=(8 + core, g), device_id_type=MESH,
        )

    def halo_right(d):
        return pltpu.make_async_remote_copy(
            src_ref=lev.at[OWN + PLANES - d], dst_ref=lev.at[OWN - d],
            send_sem=h_send.at[0, d - 1], recv_sem=h_recv.at[0, d - 1],
            device_id=(k, right), device_id_type=MESH,
        )

    def halo_left(d):
        return pltpu.make_async_remote_copy(
            src_ref=lev.at[OWN - 1 + d], dst_ref=lev.at[OWN + PLANES - 1 + d],
            send_sem=h_send.at[1, d - 1], recv_sem=h_recv.at[1, d - 1],
            device_id=(k, left), device_id_type=MESH,
        )

    def field_right(r):
        return pltpu.make_async_remote_copy(
            src_ref=fw.at[4 - r], dst_ref=fw.at[3 - r],
            send_sem=f_send.at[0, r - 1], recv_sem=f_recv.at[0, r - 1],
            device_id=(k, right), device_id_type=MESH,
        )

    def field_left(r):
        return pltpu.make_async_remote_copy(
            src_ref=fw.at[2 + r], dst_ref=fw.at[3 + r],
            send_sem=f_send.at[1, r - 1], recv_sem=f_recv.at[1, r - 1],
            device_id=(k, left), device_id_type=MESH,
        )

    def kinds(ahead):
        return pltpu.make_async_remote_copy(
            src_ref=btr, dst_ref=bt.at[pl.ds(8 - 4 * ahead, 4)],
            send_sem=b_send.at[ahead - 1], recv_sem=b_recv.at[ahead - 1],
            device_id=(lax.rem(k + ahead, 16), g), device_id_type=MESH,
        )

    order = (3, 0, 2, 1)
    plain_move = jnp.logical_and(k <= 13, jnp.logical_not(crosses))

    @pl.when(crosses)
    def _():
        move(3, lax.rem(k + 2, 16), mv_send.at[3], mv_recv.at[3]).start()
        for p in (0, 2, 1):
            to_relay(p).start()

    @pl.when(plain_move)
    def _():
        for p in order:
            move(p, lax.rem(k + 2, 16), mv_send.at[p], mv_recv.at[p]).start()

    @pl.when(k <= 13)
    def _():
        kinds(2).start()

    @pl.when(k <= 14)
    def _():
        kinds(1).start()

    @pl.when(k == 0)
    def _():
        for p in order:
            move(p, 1, mv_extra.at[p], mv_recv.at[p]).start()
        for p in order:
            pltpu.make_async_copy(inc.at[p], lev.at[OWN + p], mv_recv.at[p]).start()

    field_right(1).start()
    field_left(1).start()

    @pl.when(relays)
    def _():
        to_relay(0).wait_recv()
        from_relay().start()

    def arrive(p):
        @pl.when(k == 0)
        def _():
            pltpu.make_async_copy(inc.at[p], lev.at[OWN + p], mv_recv.at[p]).wait()

        @pl.when(k > 0)
        def _():
            move(p, lax.rem(k + 2, 16), mv_send.at[p], mv_recv.at[p]).wait_recv()

    arrive(3)
    halo_right(1).start()
    arrive(0)
    halo_left(1).start()
    arrive(2)
    halo_right(2).start()
    arrive(1)
    halo_left(2).start()
    halo_right(3).start()
    halo_left(3).start()
    halo_right(4).start()
    halo_left(4).start()

    @pl.when(k >= 1)
    def _():
        kinds(1).wait_recv()

    @pl.when(k >= 2)
    def _():
        kinds(2).wait_recv()

    row = lax.broadcasted_iota(jnp.int32, (128, 128), 0)
    lane = lax.broadcasted_iota(jnp.int32, (128, 128), 1)
    same_side = lax.rem(row, 2) == lax.div(lane, 64)
    in_use = jnp.logical_and(row < 24, same_side)
    kind_of = lax.div(lax.rem(row, 8), 2).astype(jnp.float32)

    def choose(s, carry):
        hit = jnp.logical_and(in_use, kind_of == bt[s])
        pick[s] = jnp.where(hit, 1.0, 0.0).astype(jnp.bfloat16)
        return carry

    lax.fori_loop(0, LEVELS, choose, 0)

    def load_pair(j, p_left, p_right):
        q[1 + j] = jnp.transpose(jnp.concatenate([lev[p_left], lev[p_right]], axis=0))

    load_pair(0, OWN + 1, OWN + 2)
    load_pair(1, OWN, OWN + 3)
    q[0] = pltpu.roll(q[1], 64, 1)

    def stage_steps(d, s, carry):
        restart0 = jnp.logical_and(k == 0, s == 9)
        restart1 = jnp.logical_and(k == 1, s == 5)
        level = jnp.where(jnp.logical_or(restart0, restart1), 0, s - 1)
        j = 1 + d - s
        base = level * SLOTS + j
        ax_out, ax_in, la0, la2, de0, de2 = [taps[pl.ds(n, 1)] for n in range(6)]
        along_x = []
        for n in range(4):
            rows = pl.ds(64 * n, 64)
            along_x.append(ax_out * q[base + 2, rows] + q[base + 1, rows] + ax_in * q[base, rows])
        parts = []
        for n in range(4):
            b = la0 * along_x[n - 1] + along_x[n] + la2 * along_x[(n + 1) % 4]
            pad[n, pl.ds(8, 64)] = b
            pad[n, pl.ds(7, 1)] = b[63:]
            pad[n, pl.ds(72, 1)] = b[:1]
            e = de0 * pad[n, pl.ds(7, 64)] + b + de2 * pad[n, pl.ds(9, 64)]
            e_high = e.astype(jnp.bfloat16)
            e_low = (e - e_high.astype(jnp.float32)).astype(jnp.bfloat16)
            parts.append(jnp.concatenate([e_high, e_low], axis=1))
        c = jnp.dot(jnp.concatenate(parts, axis=0), wcat[...], preferred_element_type=jnp.float32)
        factor = jnp.dot(factors[j], pick[s - 1], preferred_element_type=jnp.float32)
        fresh = (c[:, :128] + c[:, 128:]) * factor
        q[s * SLOTS + j + 1] = fresh

        @pl.when(j == 0)
        def _():
            q[s * SLOTS] = pltpu.roll(fresh, 64, 1)

        return carry

    stage_steps(0, 1, 0)

    def stage(d, carry):
        halo_right(d).wait_recv()

        @pl.when(d <= LEVELS - PLANES)
        def _():
            halo_right(d + PLANES).start()

        halo_left(d).wait_recv()

        @pl.when(d <= LEVELS - PLANES)
        def _():
            halo_left(d + PLANES).start()

        @pl.when(lax.rem(d, 4) == 1)
        def _():
            r = lax.div(d + 3, 4)
            field_right(r).wait_recv()
            field_left(r).wait_recv()

            @pl.when(r < 3)
            def _():
                field_right(r + 1).start()
                field_left(r + 1).start()

            for n in range(4):
                pair_factor(1 + d + n, 3 - r, 3 - n, 3 + r, n)

        load_pair(1 + d, OWN - d, OWN + PLANES - 1 + d)
        lax.fori_loop(1, jnp.minimum(d + 1, LEVELS) + 1, functools.partial(stage_steps, d), 0)
        return carry

    lax.fori_loop(1, LEVELS + 1, stage, 0)

    for n, owned in enumerate(((1, 2), (0, 3))):
        total = q[9 * SLOTS + 1 + n] * back_t[0, n]
        for j in range(1, 4):
            total += q[(9 + j) * SLOTS + 1 + n] * back_t[j, n]
        total = jnp.transpose(total)
        for side, p in enumerate(owned):
            for m in range(8):
                at = 64 * side + 8 * m
                part[0, m % 4, m // 4, p] = total[at:at + 4]
                part[1, m % 4, m // 4, p] = total[at + 4:at + 8]

    to_core = pltpu.make_async_remote_copy(
        src_ref=part.at[1 - core], dst_ref=r_core, send_sem=c_send, recv_sem=c_recv,
        device_id=(other_core, g), device_id_type=MESH,
    )
    to_core.start()
    for n, owned in enumerate(((1, 2), (0, 3))):
        planes = jnp.transpose(q[LEVELS * SLOTS + 1 + n])
        hand[owned[0]] = planes[:64]
        hand[owned[1]] = planes[64:]
    to_core.wait_recv()
    summed[...] = part[core] + r_core[...]

    def to_y(dy):
        return pltpu.make_async_remote_copy(
            src_ref=summed.at[lax.rem(y + dy, 4)], dst_ref=r_y.at[dy - 1],
            send_sem=y_send.at[dy - 1], recv_sem=y_recv.at[dy - 1],
            device_id=(across(dy), g), device_id_type=MESH,
        )

    for dy in (2, 1, 3):
        to_y(dy).start()
    for dy in (1, 3, 2):
        to_y(dy).wait_recv()
    s_y[...] = summed[y] + r_y[0] + r_y[1] + r_y[2]
    to_z = pltpu.make_async_remote_copy(
        src_ref=s_y.at[1 - zhi], dst_ref=r_z, send_sem=z_send, recv_sem=z_recv,
        device_id=(other_z, g), device_id_type=MESH,
    )
    to_z.start()

    def drain(d, carry):
        halo_right(d).wait_send()
        halo_left(d).wait_send()
        return carry

    lax.fori_loop(1, LEVELS + 1, drain, 0)
    for r in (1, 2, 3):
        field_right(r).wait_send()
        field_left(r).wait_send()

    @pl.when(k <= 13)
    def _():
        for p in order:
            move(p, lax.rem(k + 2, 16), mv_send.at[p], mv_recv.at[p]).wait_send()
        kinds(2).wait_send()

    @pl.when(k <= 14)
    def _():
        kinds(1).wait_send()

    @pl.when(k == 0)
    def _():
        for p in order:
            move(p, 1, mv_extra.at[p], mv_recv.at[p]).wait_send()

    @pl.when(relays)
    def _():
        from_relay().wait_send()

    to_core.wait_send()
    for dy in (1, 2, 3):
        to_y(dy).wait_send()
    to_z.wait()
    den[...] = (s_y[zhi] + r_z[...]) / contour


def per_device(
    incoming, backward, fields, block_types,
    axial_taps, lateral_taps, depth_taps, bend_diagonal, bend_coupling,
):
    n_gx = lax.axis_size("gx")
    contour = float(lax.axis_size("sec") * block_types.shape[1])
    ax, la, de = axial_taps / axial_taps[1], lateral_taps / lateral_taps[1], depth_taps / depth_taps[1]
    sides = [(ax[0], ax[2]), (ax[2], ax[0]), (la[0], la[0]), (la[2], la[2]), (de[0], de[0]), (de[2], de[2])]
    taps = jnp.stack([jnp.concatenate(pair) for pair in sides])
    kernel = jnp.diag(bend_diagonal) + bend_coupling
    turned = (kernel * (axial_taps[1] * lateral_taps[1] * depth_taps[1])[None, :]).T
    weights = jnp.concatenate(
        [jnp.pad(turned, ((0, 0), (0, ORIENT))), jnp.pad(turned, ((0, 0), (ORIENT, 0)))], axis=0
    )
    btr = jnp.broadcast_to(block_types[0].astype(jnp.float32)[:, None, None], (4, 1, 128))
    vmem = pl.BlockSpec(memory_space=pltpu.VMEM)
    dma = pltpu.SemaphoreType.DMA
    f32 = jnp.float32
    hand, den = pl.pallas_call(
        functools.partial(body, n_gx, contour),
        out_shape=(
            jax.ShapeDtypeStruct((PLANES, ORIENT, CELLS), f32),
            jax.ShapeDtypeStruct((PLANES, 4, CELLS), f32),
        ),
        in_specs=[vmem] * 6,
        out_specs=(vmem, vmem),
        scratch_shapes=[
            pltpu.VMEM((SPAN, ORIENT, CELLS), f32),
            pltpu.VMEM(((LEVELS + 1) * SLOTS, CELLS, 128), f32),
            pltpu.VMEM((4, 80, 128), f32),
            pltpu.VMEM((7, 3, PLANES, CELLS), f32),
            pltpu.VMEM((SLOTS, CELLS, 128), jnp.bfloat16),
            pltpu.VMEM((LEVELS, 1, 128), f32),
            pltpu.VMEM((LEVELS, 128, 128), jnp.bfloat16),
            pltpu.VMEM((4, 2, CELLS, 128), f32),
            pltpu.VMEM((256, 256), jnp.bfloat16),
            pltpu.VMEM((2, 4, 2, PLANES, 4, CELLS), f32),
            pltpu.VMEM((4, 2, PLANES, 4, CELLS), f32),
            pltpu.VMEM((ORIENT, CELLS), f32),
            pltpu.VMEM((4, 2, PLANES, 4, CELLS), f32),
            pltpu.VMEM((3, 2, PLANES, 4, CELLS), f32),
            pltpu.VMEM((2, PLANES, 4, CELLS), f32),
            pltpu.VMEM((PLANES, 4, CELLS), f32),
            dma((4,)), dma((4,)), dma((4,)), dma((2,)),
            dma((2, LEVELS)), dma((2, LEVELS)),
            dma((2, 3)), dma((2, 3)),
            dma((2,)), dma((2,)),
            dma((2,)),
            dma(()), dma(()),
            dma((3,)), dma((3,)),
            dma(()), dma(()),
        ],
        compiler_params=pltpu.CompilerParams(
            collective_id=0, has_side_effects=True, vmem_limit_bytes=52 << 20
        ),
        name="chain",
    )(incoming[0], backward, fields, btr, taps, weights)
    return hand[None], den


def solution(mesh):
    in_specs = (
        P("sec", "gx", None, None),
        P("sec", "gx", None, None),
        P(None, "gx", None),
        P("sec", None),
        P(), P(), P(), P(), P(),
    )
    out_specs = (P("sec", "gx", None, None), P("gx", "sec", None))
    return jax.shard_map(
        per_device, mesh=mesh, in_specs=in_specs, out_specs=out_specs, check_vma=False
    )
```

```python
import functools

import jax
import jax.numpy as jnp
from jax import lax
from jax.experimental import pallas as pl
from jax.experimental.pallas import tpu as pltpu
from jax.sharding import PartitionSpec as P

MESH = pl.DeviceIdType.MESH
PLANES = 4
LEVELS = 12
SPAN = PLANES + 2 * LEVELS
OWN = LEVELS
ORIENT = 64
CELLS = 256
SLOTS = 15


def body(
    n_gx, contour,
    inc_hbm, back, fld, btr_hbm, ax_hbm, la_hbm, de_hbm, diagonal_hbm, coupling_hbm,
    hand, den,
    inc, btr, ax_taps, la_taps, de_taps, diagonal, coupling,
    lev, q, pad, fw, factors, bt, pick, scaled, held, back_t, wcat, taps, part, summed, relay, r_core, r_y, s_y, r_z,
    mv_send, mv_recv, mv_extra, relay_sem, h_send, h_recv, f_send, f_recv, b_send, b_recv,
    loc, c_send, c_recv, y_send, y_recv, z_send, z_recv,
):
    k = lax.axis_index("sec")
    g = lax.axis_index("gx")
    core = lax.rem(k, 2)
    y = lax.rem(lax.div(k, 2), 4)
    zhi = lax.div(k, 8)
    right = lax.rem(g + 1, n_gx)
    left = lax.rem(g + n_gx - 1, n_gx)
    other_core = k + 1 - 2 * core
    other_z = lax.rem(k + 8, 16)
    relays = k < 6
    crosses = jnp.logical_and(k >= 6, k <= 7)

    def across(dy):
        return 8 * zhi + 2 * lax.rem(y + dy, 4) + core

    fetches = [
        pltpu.make_async_copy(src, dst, loc.at[n])
        for n, (src, dst) in enumerate((
            (inc_hbm.at[0], inc), (btr_hbm, btr), (fld, fw.at[3]), (ax_hbm, ax_taps), (la_hbm, la_taps),
            (de_hbm, de_taps), (diagonal_hbm, diagonal), (coupling_hbm, coupling), (back, held),
        ))
    ]
    for fetch in fetches:
        fetch.start()
    bt[...] = jnp.zeros((3, 1, 4), jnp.int32)
    barrier = pltpu.get_barrier_semaphore()
    sections = [lax.rem(k + n, 16) for n in (1, 2, 14, 15)]
    sections += [other_core, other_z] + [across(n) for n in (1, 2, 3)]
    for n in sections:
        pl.semaphore_signal(barrier, inc=1, device_id=(n, g), device_id_type=MESH)
    for n in (left, right):
        pl.semaphore_signal(barrier, inc=1, device_id=(k, n), device_id_type=MESH)

    @pl.when(jnp.logical_and(k >= 8, k <= 9))
    def _():
        for n in (4, 6):
            pl.semaphore_signal(barrier, inc=1, device_id=(k - n, g), device_id_type=MESH)

    for fetch in fetches[:-1]:
        fetch.wait()
    ax, la, de = [t[...] for t in (ax_taps, la_taps, de_taps)]

    def lanes(t, n, m):
        return jnp.concatenate([t[n:n + 1] / t[1:2], t[m:m + 1] / t[1:2]], axis=1)

    for n, one in enumerate(
        (lanes(ax, 0, 2), lanes(ax, 2, 0), lanes(la, 0, 0), lanes(la, 2, 2), lanes(de, 0, 0), lanes(de, 2, 2))
    ):
        taps[pl.ds(n, 1)] = one
    square = (ORIENT, ORIENT)
    on_diagonal = lax.broadcasted_iota(jnp.int32, square, 0) == lax.broadcasted_iota(jnp.int32, square, 1)
    kernel = coupling[...] + jnp.where(on_diagonal, jnp.broadcast_to(diagonal[...], square), 0.0)
    turned = jnp.transpose(kernel * (ax[1:2] * la[1:2] * de[1:2]))
    none = jnp.zeros(square, jnp.float32)
    full = jnp.concatenate(
        [jnp.concatenate([turned, none], axis=1), jnp.concatenate([none, turned], axis=1)], axis=0
    )
    high = full.astype(jnp.bfloat16)
    low = (full - high.astype(jnp.float32)).astype(jnp.bfloat16)
    for n in range(2):
        wcat[pl.ds(128 * n, 128), pl.ds(0, 128)] = high
        wcat[pl.ds(128 * n, 128), pl.ds(128, 128)] = low
    def pair_factor(j, slab_left, row_left, slab_right, row_right):
        rows = []
        for t in range(3):
            rows.append(jnp.exp(-fw[slab_left, t, pl.ds(row_left, 1)]))
            rows.append(jnp.exp(-fw[slab_right, t, pl.ds(row_right, 1)]))
        rows = jnp.concatenate(rows + [jnp.zeros((2, CELLS), jnp.float32)], axis=0)
        first = rows.astype(jnp.bfloat16).astype(jnp.float32)
        rest = rows - first
        second = rest.astype(jnp.bfloat16).astype(jnp.float32)
        stack = [first, second, rest - second, jnp.zeros((104, CELLS), jnp.float32)]
        factors[j] = jnp.transpose(jnp.concatenate(stack, axis=0)).astype(jnp.bfloat16)

    pair_factor(0, 3, 1, 3, 2)
    pair_factor(1, 3, 0, 3, 3)

    @pl.when(jnp.logical_and(k >= 2, k <= 5))
    def _():
        pl.semaphore_wait(barrier, 12)

    @pl.when(jnp.logical_or(k < 2, k > 5))
    def _():
        pl.semaphore_wait(barrier, 11)

    def move(p, target, send, recv):
        return pltpu.make_async_remote_copy(
            src_ref=inc.at[p], dst_ref=lev.at[OWN + p], send_sem=send, recv_sem=recv,
            device_id=(target, g), device_id_type=MESH,
        )

    def to_relay(p):
        return pltpu.make_async_remote_copy(
            src_ref=inc.at[p], dst_ref=relay, send_sem=mv_send.at[p], recv_sem=relay_sem.at[0],
            device_id=(2 * p + core, g), device_id_type=MESH,
        )

    def from_relay():
        return pltpu.make_async_remote_copy(
            src_ref=relay, dst_ref=lev.at[OWN + y], send_sem=relay_sem.at[1], recv_sem=mv_recv.at[y],
            device_id=(8 + core, g), device_id_type=MESH,
        )

    def halo_right(d):
        return pltpu.make_async_remote_copy(
            src_ref=lev.at[OWN + PLANES - d], dst_ref=lev.at[OWN - d],
            send_sem=h_send.at[0, d - 1], recv_sem=h_recv.at[0, d - 1],
            device_id=(k, right), device_id_type=MESH,
        )

    def halo_left(d):
        return pltpu.make_async_remote_copy(
            src_ref=lev.at[OWN - 1 + d], dst_ref=lev.at[OWN + PLANES - 1 + d],
            send_sem=h_send.at[1, d - 1], recv_sem=h_recv.at[1, d - 1],
            device_id=(k, left), device_id_type=MESH,
        )

    def field_right(r):
        return pltpu.make_async_remote_copy(
            src_ref=fw.at[4 - r], dst_ref=fw.at[3 - r],
            send_sem=f_send.at[0, r - 1], recv_sem=f_recv.at[0, r - 1],
            device_id=(k, right), device_id_type=MESH,
        )

    def field_left(r):
        return pltpu.make_async_remote_copy(
            src_ref=fw.at[2 + r], dst_ref=fw.at[3 + r],
            send_sem=f_send.at[1, r - 1], recv_sem=f_recv.at[1, r - 1],
            device_id=(k, left), device_id_type=MESH,
        )

    def kinds(ahead):
        return pltpu.make_async_remote_copy(
            src_ref=btr, dst_ref=bt.at[2 - ahead],
            send_sem=b_send.at[ahead - 1], recv_sem=b_recv.at[ahead - 1],
            device_id=(lax.rem(k + ahead, 16), g), device_id_type=MESH,
        )

    order = (3, 0, 2, 1)
    plain_move = jnp.logical_and(k <= 13, jnp.logical_not(crosses))

    @pl.when(crosses)
    def _():
        move(3, lax.rem(k + 2, 16), mv_send.at[3], mv_recv.at[3]).start()
        for p in (0, 2, 1):
            to_relay(p).start()

    @pl.when(plain_move)
    def _():
        for p in order:
            move(p, lax.rem(k + 2, 16), mv_send.at[p], mv_recv.at[p]).start()

    @pl.when(k <= 13)
    def _():
        kinds(2).start()

    @pl.when(k <= 14)
    def _():
        kinds(1).start()

    @pl.when(k == 0)
    def _():
        for p in order:
            move(p, 1, mv_extra.at[p], mv_recv.at[p]).start()
        for p in order:
            pltpu.make_async_copy(inc.at[p], lev.at[OWN + p], mv_recv.at[p]).start()

    field_right(1).start()
    field_left(1).start()

    fetches[-1].wait()
    for j in range(4):
        for n, (p_left, p_right) in enumerate(((1, 2), (0, 3))):
            both = jnp.concatenate([held[j, p_left], held[j, p_right]], axis=0)
            back_t[j, n] = jnp.transpose(both.astype(jnp.float32))

    @pl.when(relays)
    def _():
        to_relay(0).wait_recv()
        from_relay().start()

    def arrive(p):
        @pl.when(k == 0)
        def _():
            pltpu.make_async_copy(inc.at[p], lev.at[OWN + p], mv_recv.at[p]).wait()

        @pl.when(k > 0)
        def _():
            move(p, lax.rem(k + 2, 16), mv_send.at[p], mv_recv.at[p]).wait_recv()

    arrive(3)
    halo_right(1).start()
    arrive(0)
    halo_left(1).start()
    arrive(2)
    halo_right(2).start()
    arrive(1)
    halo_left(2).start()
    for d in (3, 4):
        halo_right(d).start()
        halo_left(d).start()

    @pl.when(k >= 1)
    def _():
        kinds(1).wait_recv()

    @pl.when(k >= 2)
    def _():
        kinds(2).wait_recv()

    row = lax.broadcasted_iota(jnp.int32, (128, 128), 0)
    lane = lax.broadcasted_iota(jnp.int32, (128, 128), 1)
    same_side = lax.rem(row, 2) == lax.div(lane, 64)
    in_use = jnp.logical_and(row < 24, same_side)
    kind_of = lax.div(lax.rem(row, 8), 2)
    step_of = lax.broadcasted_iota(jnp.int32, (1, 4), 1)

    for s in range(LEVELS):
        own = btr[...] if s >= 8 else bt[s // 4]
        kind = jnp.sum(jnp.where(step_of == s % 4, own, 0), axis=1, keepdims=True)
        hit = jnp.logical_and(in_use, kind_of == jnp.broadcast_to(kind, (128, 128)))
        pick[s] = jnp.where(hit, 1.0, 0.0).astype(jnp.bfloat16)

    def load_pair(j, p_left, p_right):
        q[1 + j] = jnp.transpose(jnp.concatenate([lev[p_left], lev[p_right]], axis=0))

    load_pair(0, OWN + 1, OWN + 2)
    load_pair(1, OWN, OWN + 3)
    q[0] = pltpu.roll(q[1], 64, 1)

    def stage_steps(d, s, carry):
        restart0 = jnp.logical_and(k == 0, s == 9)
        restart1 = jnp.logical_and(k == 1, s == 5)
        level = jnp.where(jnp.logical_or(restart0, restart1), 0, s - 1)
        j = 1 + d - s
        base = level * SLOTS + j
        ax_out, ax_in, la0, la2, de0, de2 = [taps[pl.ds(n, 1)] for n in range(6)]
        scaled[...] = jnp.dot(factors[j], pick[s - 1], preferred_element_type=jnp.float32)
        along_x = []
        for n in range(4):
            rows = pl.ds(64 * n, 64)
            along_x.append(ax_out * q[base + 2, rows] + q[base + 1, rows] + ax_in * q[base, rows])
        parts = []
        for n in range(4):
            b = la0 * along_x[n - 1] + along_x[n] + la2 * along_x[(n + 1) % 4]
            pad[n, pl.ds(8, 64)] = b
            pad[n, pl.ds(7, 1)] = b[63:]
            pad[n, pl.ds(72, 1)] = b[:1]
            e = de0 * pad[n, pl.ds(7, 64)] + b + de2 * pad[n, pl.ds(9, 64)]
            e_high = e.astype(jnp.bfloat16)
            e_low = (e - e_high.astype(jnp.float32)).astype(jnp.bfloat16)
            parts.append(jnp.concatenate([e_high, e_low], axis=1))
        c = jnp.dot(jnp.concatenate(parts, axis=0), wcat[...], preferred_element_type=jnp.float32)
        fresh = (c[:, :128] + c[:, 128:]) * scaled[...]
        q[s * SLOTS + j + 1] = fresh

        @pl.when(j == 0)
        def _():
            q[s * SLOTS] = pltpu.roll(q[s * SLOTS + 1], 64, 1)

        return carry

    stage_steps(0, 1, 0)

    def stage(d, carry):
        halo_right(d).wait_recv()

        @pl.when(d <= LEVELS - PLANES)
        def _():
            halo_right(d + PLANES).start()

        halo_left(d).wait_recv()

        @pl.when(d <= LEVELS - PLANES)
        def _():
            halo_left(d + PLANES).start()

        @pl.when(lax.rem(d, 4) == 1)
        def _():
            r = lax.div(d + 3, 4)
            field_right(r).wait_recv()
            field_left(r).wait_recv()

            @pl.when(r < 3)
            def _():
                field_right(r + 1).start()
                field_left(r + 1).start()

            for n in range(4):
                pair_factor(1 + d + n, 3 - r, 3 - n, 3 + r, n)

        load_pair(1 + d, OWN - d, OWN + PLANES - 1 + d)
        lax.fori_loop(1, jnp.minimum(d + 1, LEVELS) + 1, functools.partial(stage_steps, d), 0)
        return carry

    lax.fori_loop(1, LEVELS + 1, stage, 0)

    for n, owned in enumerate(((1, 2), (0, 3))):
        total = q[9 * SLOTS + 1 + n] * back_t[0, n]
        for j in range(1, 4):
            total += q[(9 + j) * SLOTS + 1 + n] * back_t[j, n]
        total = jnp.transpose(total)
        for side, p in enumerate(owned):
            for m in range(8):
                at = 64 * side + 8 * m
                part[0, m % 4, m // 4, p] = total[at:at + 4]
                part[1, m % 4, m // 4, p] = total[at + 4:at + 8]

    to_core = pltpu.make_async_remote_copy(
        src_ref=part.at[1 - core], dst_ref=r_core, send_sem=c_send, recv_sem=c_recv,
        device_id=(other_core, g), device_id_type=MESH,
    )
    to_core.start()
    for n, owned in enumerate(((1, 2), (0, 3))):
        planes = jnp.transpose(q[LEVELS * SLOTS + 1 + n])
        hand[owned[0]] = planes[:64]
        hand[owned[1]] = planes[64:]
    to_core.wait_recv()
    summed[...] = part[core] + r_core[...]

    def to_y(dy):
        return pltpu.make_async_remote_copy(
            src_ref=summed.at[lax.rem(y + dy, 4)], dst_ref=r_y.at[dy - 1],
            send_sem=y_send.at[dy - 1], recv_sem=y_recv.at[dy - 1],
            device_id=(across(dy), g), device_id_type=MESH,
        )

    for dy in (2, 1, 3):
        to_y(dy).start()
    for dy in (1, 3, 2):
        to_y(dy).wait_recv()
    s_y[...] = summed[y] + r_y[0] + r_y[1] + r_y[2]
    to_z = pltpu.make_async_remote_copy(
        src_ref=s_y.at[1 - zhi], dst_ref=r_z, send_sem=z_send, recv_sem=z_recv,
        device_id=(other_z, g), device_id_type=MESH,
    )
    to_z.start()

    def drain(d, carry):
        halo_right(d).wait_send()
        halo_left(d).wait_send()
        return carry

    lax.fori_loop(1, LEVELS + 1, drain, 0)
    for r in (1, 2, 3):
        field_right(r).wait_send()
        field_left(r).wait_send()

    @pl.when(k <= 13)
    def _():
        for p in order:
            move(p, lax.rem(k + 2, 16), mv_send.at[p], mv_recv.at[p]).wait_send()
        kinds(2).wait_send()

    @pl.when(k <= 14)
    def _():
        kinds(1).wait_send()

    @pl.when(k == 0)
    def _():
        for p in order:
            move(p, 1, mv_extra.at[p], mv_recv.at[p]).wait_send()

    @pl.when(relays)
    def _():
        from_relay().wait_send()

    to_core.wait_send()
    for dy in (1, 2, 3):
        to_y(dy).wait_send()
    to_z.wait()
    den[...] = (s_y[zhi] + r_z[...]) / contour


def per_device(
    incoming, backward, fields, block_types,
    axial_taps, lateral_taps, depth_taps, bend_diagonal, bend_coupling,
):
    n_gx = lax.axis_size("gx")
    contour = float(lax.axis_size("sec") * block_types.shape[1])
    vmem = pl.BlockSpec(memory_space=pltpu.VMEM)
    hbm = pl.BlockSpec(memory_space=pltpu.HBM)
    dma = pltpu.SemaphoreType.DMA
    f32 = jnp.float32
    hand, den = pl.pallas_call(
        functools.partial(body, n_gx, contour),
        out_shape=(
            jax.ShapeDtypeStruct((PLANES, ORIENT, CELLS), f32),
            jax.ShapeDtypeStruct((PLANES, 4, CELLS), f32),
        ),
        in_specs=[hbm] * 9,
        out_specs=(vmem, vmem),
        scratch_shapes=[
            pltpu.VMEM((PLANES, ORIENT, CELLS), f32),
            pltpu.VMEM((1, 4), jnp.int32),
            pltpu.VMEM((3, ORIENT), f32),
            pltpu.VMEM((3, ORIENT), f32),
            pltpu.VMEM((3, ORIENT), f32),
            pltpu.VMEM((1, ORIENT), f32),
            pltpu.VMEM((ORIENT, ORIENT), f32),
            pltpu.VMEM((SPAN, ORIENT, CELLS), f32),
            pltpu.VMEM(((LEVELS + 1) * SLOTS, CELLS, 128), f32),
            pltpu.VMEM((4, 80, 128), f32),
            pltpu.VMEM((7, 3, PLANES, CELLS), f32),
            pltpu.VMEM((SLOTS, CELLS, 128), jnp.bfloat16),
            pltpu.VMEM((3, 1, 4), jnp.int32),
            pltpu.VMEM((LEVELS, 128, 128), jnp.bfloat16),
            pltpu.VMEM((CELLS, 128), f32),
            pltpu.VMEM((4, PLANES, ORIENT, CELLS), jnp.bfloat16),
            pltpu.VMEM((4, 2, CELLS, 128), f32),
            pltpu.VMEM((256, 256), jnp.bfloat16),
            pltpu.VMEM((8, 128), f32),
            pltpu.VMEM((2, 4, 2, PLANES, 4, CELLS), f32),
            pltpu.VMEM((4, 2, PLANES, 4, CELLS), f32),
            pltpu.VMEM((ORIENT, CELLS), f32),
            pltpu.VMEM((4, 2, PLANES, 4, CELLS), f32),
            pltpu.VMEM((3, 2, PLANES, 4, CELLS), f32),
            pltpu.VMEM((2, PLANES, 4, CELLS), f32),
            pltpu.VMEM((PLANES, 4, CELLS), f32),
            dma((4,)), dma((4,)), dma((4,)), dma((2,)),
            dma((2, LEVELS)), dma((2, LEVELS)),
            dma((2, 3)), dma((2, 3)),
            dma((2,)), dma((2,)),
            dma((9,)),
            dma(()), dma(()),
            dma((3,)), dma((3,)),
            dma(()), dma(()),
        ],
        compiler_params=pltpu.CompilerParams(
            collective_id=0, has_side_effects=True, vmem_limit_bytes=67043328
        ),
        name="chain",
    )(
        incoming, backward, fields, block_types,
        axial_taps, lateral_taps, depth_taps, bend_diagonal[None], bend_coupling,
    )
    return hand[None], den


def solution(mesh):
    in_specs = (
        P("sec", "gx", None, None),
        P("sec", "gx", None, None),
        P(None, "gx", None),
        P("sec", None),
        P(), P(), P(), P(), P(),
    )
    out_specs = (P("sec", "gx", None, None), P("gx", "sec", None))
    return jax.shard_map(
        per_device, mesh=mesh, in_specs=in_specs, out_specs=out_specs, check_vma=False
    )
```

```python
import functools

import jax
import jax.numpy as jnp
from jax import lax
from jax.experimental import pallas as pl
from jax.experimental.pallas import tpu as pltpu
from jax.sharding import PartitionSpec as P

MESH = pl.DeviceIdType.MESH
PLANES = 4
LEVELS = 12
SPAN = PLANES + 2 * LEVELS
OWN = LEVELS
ORIENT = 64
CELLS = 256
SLOTS = 15


def body(
    n_gx, contour,
    inc_hbm, back, fld, btr_hbm, ax_hbm, la_hbm, de_hbm, diagonal_hbm, coupling_hbm,
    hand, den,
    inc, btr, ax_taps, la_taps, de_taps, diagonal, coupling,
    lev, q, pad, fw, factors, bt, pick, scaled, along_x, held, back_t, wcat, taps, part, summed, relay, r_core, r_y, s_y, r_z,
    mv_send, mv_recv, mv_extra, relay_sem, s_send, h_send, h_recv, f_send, f_recv, b_send, b_recv,
    loc, c_send, c_recv, y_send, y_recv, z_send, z_recv,
):
    k = lax.axis_index("sec")
    g = lax.axis_index("gx")
    core = lax.rem(k, 2)
    y = lax.rem(lax.div(k, 2), 4)
    zhi = lax.div(k, 8)
    right = lax.rem(g + 1, n_gx)
    left = lax.rem(g + n_gx - 1, n_gx)
    other_core = k + 1 - 2 * core
    other_z = lax.rem(k + 8, 16)
    relays = k < 6
    crosses = jnp.logical_and(k >= 6, k <= 7)
    at_run = lax.rem(g, 8)
    reach = LEVELS - 8 * (k == 0).astype(jnp.int32) - 4 * (k == 1).astype(jnp.int32)
    crossed = jnp.logical_and(k >= 8, k <= 9)
    sends_right = jnp.logical_not(jnp.logical_and(crossed, at_run == 7))
    sends_left = jnp.logical_not(jnp.logical_and(crossed, at_run == 0))
    skips_right = jnp.logical_and(crosses, at_run == 7)
    skips_left = jnp.logical_and(crosses, at_run == 0)

    def across(dy):
        return 8 * zhi + 2 * lax.rem(y + dy, 4) + core

    fetches = [
        pltpu.make_async_copy(src, dst, loc.at[n])
        for n, (src, dst) in enumerate((
            (inc_hbm.at[0], inc), (btr_hbm, btr), (fld, fw.at[3]), (ax_hbm, ax_taps), (la_hbm, la_taps),
            (de_hbm, de_taps), (diagonal_hbm, diagonal), (coupling_hbm, coupling), (back, held),
        ))
    ]
    for fetch in fetches:
        fetch.start()
    bt[...] = jnp.zeros((3, 1, 4), jnp.int32)
    barrier = pltpu.get_barrier_semaphore()
    sections = [lax.rem(k + n, 16) for n in (1, 2, 14, 15)]
    sections += [other_core, other_z] + [across(n) for n in (1, 2, 3)]
    for n in sections:
        pl.semaphore_signal(barrier, inc=1, device_id=(n, g), device_id_type=MESH)
    for n in (left, right):
        pl.semaphore_signal(barrier, inc=1, device_id=(k, n), device_id_type=MESH)

    @pl.when(jnp.logical_and(k >= 8, k <= 9))
    def _():
        for n in (4, 6):
            pl.semaphore_signal(barrier, inc=1, device_id=(k - n, g), device_id_type=MESH)

        @pl.when(at_run == 0)
        def _():
            pl.semaphore_signal(barrier, inc=1, device_id=(k - 2, left), device_id_type=MESH)

        @pl.when(at_run == 7)
        def _():
            pl.semaphore_signal(barrier, inc=1, device_id=(k - 2, right), device_id_type=MESH)

    for fetch in fetches[:-1]:
        fetch.wait()
    ax, la, de = [t[...] for t in (ax_taps, la_taps, de_taps)]

    def lanes(t, n, m):
        return jnp.concatenate([t[n:n + 1] / t[1:2], t[m:m + 1] / t[1:2]], axis=1)

    for n, one in enumerate(
        (lanes(ax, 0, 2), lanes(ax, 2, 0), lanes(la, 0, 0), lanes(la, 2, 2), lanes(de, 0, 0), lanes(de, 2, 2))
    ):
        taps[pl.ds(n, 1)] = one
    square = (ORIENT, ORIENT)
    on_diagonal = lax.broadcasted_iota(jnp.int32, square, 0) == lax.broadcasted_iota(jnp.int32, square, 1)
    kernel = coupling[...] + jnp.where(on_diagonal, jnp.broadcast_to(diagonal[...], square), 0.0)
    turned = jnp.transpose(kernel * (ax[1:2] * la[1:2] * de[1:2]))
    none = jnp.zeros(square, jnp.float32)
    full = jnp.concatenate(
        [jnp.concatenate([turned, none], axis=1), jnp.concatenate([none, turned], axis=1)], axis=0
    )
    high = full.astype(jnp.bfloat16)
    low = (full - high.astype(jnp.float32)).astype(jnp.bfloat16)
    for n in range(2):
        wcat[pl.ds(128 * n, 128), pl.ds(0, 128)] = high
        wcat[pl.ds(128 * n, 128), pl.ds(128, 128)] = low
    def pair_factor(j, slab_left, row_left, slab_right, row_right):
        rows = []
        for t in range(3):
            rows.append(jnp.exp(-fw[slab_left, t, pl.ds(row_left, 1)]))
            rows.append(jnp.exp(-fw[slab_right, t, pl.ds(row_right, 1)]))
        rows = jnp.concatenate(rows + [jnp.zeros((2, CELLS), jnp.float32)], axis=0)
        first = rows.astype(jnp.bfloat16).astype(jnp.float32)
        rest = rows - first
        second = rest.astype(jnp.bfloat16).astype(jnp.float32)
        stack = [first, second, rest - second, jnp.zeros((104, CELLS), jnp.float32)]
        factors[j] = jnp.transpose(jnp.concatenate(stack, axis=0)).astype(jnp.bfloat16)

    pair_factor(0, 3, 1, 3, 2)
    pair_factor(1, 3, 0, 3, 3)

    skips = jnp.logical_or(skips_right, skips_left)
    one_more = jnp.logical_or(jnp.logical_and(k >= 2, k <= 5), skips)

    @pl.when(one_more)
    def _():
        pl.semaphore_wait(barrier, 12)

    @pl.when(jnp.logical_not(one_more))
    def _():
        pl.semaphore_wait(barrier, 11)

    def move(p, target, send, recv):
        return pltpu.make_async_remote_copy(
            src_ref=inc.at[p], dst_ref=lev.at[OWN + p], send_sem=send, recv_sem=recv,
            device_id=(target, g), device_id_type=MESH,
        )

    def to_relay(p):
        return pltpu.make_async_remote_copy(
            src_ref=inc.at[p], dst_ref=relay, send_sem=mv_send.at[p], recv_sem=relay_sem.at[0],
            device_id=(2 * p + core, g), device_id_type=MESH,
        )

    def from_relay():
        return pltpu.make_async_remote_copy(
            src_ref=relay, dst_ref=lev.at[OWN + y], send_sem=relay_sem.at[1], recv_sem=mv_recv.at[y],
            device_id=(8 + core, g), device_id_type=MESH,
        )

    def halo_right(d):
        return pltpu.make_async_remote_copy(
            src_ref=lev.at[OWN + PLANES - d], dst_ref=lev.at[OWN - d],
            send_sem=h_send.at[0, d - 1], recv_sem=h_recv.at[0, d - 1],
            device_id=(k, right), device_id_type=MESH,
        )

    def halo_left(d):
        return pltpu.make_async_remote_copy(
            src_ref=lev.at[OWN - 1 + d], dst_ref=lev.at[OWN + PLANES - 1 + d],
            send_sem=h_send.at[1, d - 1], recv_sem=h_recv.at[1, d - 1],
            device_id=(k, left), device_id_type=MESH,
        )

    def field_right(r):
        return pltpu.make_async_remote_copy(
            src_ref=fw.at[4 - r], dst_ref=fw.at[3 - r],
            send_sem=f_send.at[0, r - 1], recv_sem=f_recv.at[0, r - 1],
            device_id=(k, right), device_id_type=MESH,
        )

    def field_left(r):
        return pltpu.make_async_remote_copy(
            src_ref=fw.at[2 + r], dst_ref=fw.at[3 + r],
            send_sem=f_send.at[1, r - 1], recv_sem=f_recv.at[1, r - 1],
            device_id=(k, left), device_id_type=MESH,
        )

    def kinds(ahead):
        return pltpu.make_async_remote_copy(
            src_ref=btr, dst_ref=bt.at[2 - ahead],
            send_sem=b_send.at[ahead - 1], recv_sem=b_recv.at[ahead - 1],
            device_id=(lax.rem(k + ahead, 16), g), device_id_type=MESH,
        )

    def skip_right(p):
        d = PLANES - p
        return pltpu.make_async_remote_copy(
            src_ref=inc.at[p], dst_ref=lev.at[OWN - d], send_sem=s_send.at[p], recv_sem=h_recv.at[0, d - 1],
            device_id=(k + 2, right), device_id_type=MESH,
        )

    def skip_left(p):
        d = p + 1
        return pltpu.make_async_remote_copy(
            src_ref=inc.at[p], dst_ref=lev.at[OWN + PLANES - 1 + d], send_sem=s_send.at[p],
            recv_sem=h_recv.at[1, d - 1],
            device_id=(k + 2, left), device_id_type=MESH,
        )

    order = (3, 0, 2, 1)
    plain_move = jnp.logical_and(k <= 13, jnp.logical_not(crosses))

    @pl.when(crosses)
    def _():
        move(3, lax.rem(k + 2, 16), mv_send.at[3], mv_recv.at[3]).start()
        for p in (0, 2, 1):
            to_relay(p).start()

    @pl.when(skips_right)
    def _():
        for p in (3, 2, 1, 0):
            skip_right(p).start()

    @pl.when(skips_left)
    def _():
        for p in (0, 1, 2, 3):
            skip_left(p).start()

    @pl.when(plain_move)
    def _():
        for p in order:
            move(p, lax.rem(k + 2, 16), mv_send.at[p], mv_recv.at[p]).start()

    @pl.when(k <= 13)
    def _():
        kinds(2).start()

    @pl.when(k <= 14)
    def _():
        kinds(1).start()

    @pl.when(k == 0)
    def _():
        for p in order:
            move(p, 1, mv_extra.at[p], mv_recv.at[p]).start()
        for p in order:
            pltpu.make_async_copy(inc.at[p], lev.at[OWN + p], mv_recv.at[p]).start()

    field_right(1).start()
    field_left(1).start()

    @pl.when(relays)
    def _():
        to_relay(0).wait_recv()
        from_relay().start()

    fetches[-1].wait()
    for j in range(4):
        for n, (p_left, p_right) in enumerate(((1, 2), (0, 3))):
            both = jnp.concatenate([held[j, p_left], held[j, p_right]], axis=0)
            back_t[j, n] = jnp.transpose(both.astype(jnp.float32))

    def arrive(p):
        @pl.when(k == 0)
        def _():
            pltpu.make_async_copy(inc.at[p], lev.at[OWN + p], mv_recv.at[p]).wait()

        @pl.when(k > 0)
        def _():
            move(p, lax.rem(k + 2, 16), mv_send.at[p], mv_recv.at[p]).wait_recv()

    def send_right(d):
        @pl.when(sends_right)
        def _():
            halo_right(d).start()

    def send_left(d):
        @pl.when(sends_left)
        def _():
            halo_left(d).start()

    arrive(3)
    send_right(1)
    arrive(0)
    send_left(1)
    arrive(2)
    send_right(2)
    arrive(1)
    send_left(2)
    for d in (3, 4):
        send_right(d)
        send_left(d)

    @pl.when(k >= 1)
    def _():
        kinds(1).wait_recv()

    @pl.when(k >= 2)
    def _():
        kinds(2).wait_recv()

    row = lax.broadcasted_iota(jnp.int32, (128, 128), 0)
    lane = lax.broadcasted_iota(jnp.int32, (128, 128), 1)
    same_side = lax.rem(row, 2) == lax.div(lane, 64)
    in_use = jnp.logical_and(row < 24, same_side)
    kind_of = lax.div(lax.rem(row, 8), 2)
    step_of = lax.broadcasted_iota(jnp.int32, (1, 4), 1)

    for s in range(LEVELS):
        own = btr[...] if s >= 8 else bt[s // 4]
        kind = jnp.sum(jnp.where(step_of == s % 4, own, 0), axis=1, keepdims=True)
        hit = jnp.logical_and(in_use, kind_of == jnp.broadcast_to(kind, (128, 128)))
        pick[s] = jnp.where(hit, 1.0, 0.0).astype(jnp.bfloat16)

    def load_pair(j, p_left, p_right):
        q[1 + j] = jnp.transpose(jnp.concatenate([lev[p_left], lev[p_right]], axis=0))

    load_pair(0, OWN + 1, OWN + 2)
    load_pair(1, OWN, OWN + 3)
    q[0] = pltpu.roll(q[1], 64, 1)

    ax_out, ax_in, la0, la2, de0, de2 = [taps[pl.ds(n, 1)] for n in range(6)]

    def mix(outer, at):
        along_x[...] = ax_out * outer + q[at] + ax_in * q[at - 1]

    def stage_steps(d, s, carry):
        j = 1 + d - s
        at = s * SLOTS + j
        scaled[...] = jnp.dot(factors[j], pick[s - 1], preferred_element_type=jnp.float32)
        parts = []
        for n in range(4):
            before, here, after = [along_x[pl.ds(64 * (m % 4), 64)] for m in (n - 1, n, n + 1)]
            b = la0 * before + here + la2 * after
            pad[n, pl.ds(8, 64)] = b
            pad[n, pl.ds(7, 1)] = b[63:]
            pad[n, pl.ds(72, 1)] = b[:1]
            e = de0 * pad[n, pl.ds(7, 64)] + b + de2 * pad[n, pl.ds(9, 64)]
            e_high = e.astype(jnp.bfloat16)
            e_low = (e - e_high.astype(jnp.float32)).astype(jnp.bfloat16)
            parts.append(jnp.concatenate([e_high, e_low], axis=1))
        c = jnp.dot(jnp.concatenate(parts, axis=0), wcat[...], preferred_element_type=jnp.float32)
        fresh = (c[:, :128] + c[:, 128:]) * scaled[...]
        mix(fresh, at)
        q[at + 1] = fresh
        restart0 = jnp.logical_and(k == 0, s == 8)
        restart1 = jnp.logical_and(k == 1, s == 4)

        @pl.when(jnp.logical_and(jnp.logical_or(restart0, restart1), j >= 1))
        def _():
            mix(q[j + 1], j)

        @pl.when(j == 0)
        def _():
            q[s * SLOTS] = pltpu.roll(q[s * SLOTS + 1], 64, 1)

        return carry

    mix(q[2], 1)
    stage_steps(0, 1, 0)

    def stage(d, carry):
        @pl.when(d <= reach)
        def _():
            halo_right(d).wait_recv()

        @pl.when(d <= reach - PLANES)
        def _():
            halo_right(d + PLANES).start()

        @pl.when(d <= reach)
        def _():
            halo_left(d).wait_recv()

        @pl.when(d <= reach - PLANES)
        def _():
            halo_left(d + PLANES).start()

        @pl.when(lax.rem(d, 4) == 1)
        def _():
            r = lax.div(d + 3, 4)
            field_right(r).wait_recv()
            field_left(r).wait_recv()

            @pl.when(r < 3)
            def _():
                field_right(r + 1).start()
                field_left(r + 1).start()

            for n in range(4):
                pair_factor(1 + d + n, 3 - r, 3 - n, 3 + r, n)

        load_pair(1 + d, OWN - d, OWN + PLANES - 1 + d)
        mix(q[d + 2], d + 1)
        lax.fori_loop(1, jnp.minimum(d + 1, LEVELS) + 1, functools.partial(stage_steps, d), 0)
        return carry

    lax.fori_loop(1, LEVELS + 1, stage, 0)

    for n, owned in enumerate(((1, 2), (0, 3))):
        total = q[9 * SLOTS + 1 + n] * back_t[0, n]
        for j in range(1, 4):
            total += q[(9 + j) * SLOTS + 1 + n] * back_t[j, n]
        total = jnp.transpose(total)
        for side, p in enumerate(owned):
            for m in range(8):
                at = 64 * side + 8 * m
                part[0, m % 4, m // 4, p] = total[at:at + 4]
                part[1, m % 4, m // 4, p] = total[at + 4:at + 8]

    to_core = pltpu.make_async_remote_copy(
        src_ref=part.at[1 - core], dst_ref=r_core, send_sem=c_send, recv_sem=c_recv,
        device_id=(other_core, g), device_id_type=MESH,
    )
    to_core.start()
    for n, owned in enumerate(((1, 2), (0, 3))):
        planes = jnp.transpose(q[LEVELS * SLOTS + 1 + n])
        hand[owned[0]] = planes[:64]
        hand[owned[1]] = planes[64:]
    to_core.wait_recv()
    summed[...] = part[core] + r_core[...]

    def to_y(dy):
        return pltpu.make_async_remote_copy(
            src_ref=summed.at[lax.rem(y + dy, 4)], dst_ref=r_y.at[dy - 1],
            send_sem=y_send.at[dy - 1], recv_sem=y_recv.at[dy - 1],
            device_id=(across(dy), g), device_id_type=MESH,
        )

    for dy in (2, 1, 3):
        to_y(dy).start()
    for dy in (1, 3, 2):
        to_y(dy).wait_recv()
    s_y[...] = summed[y] + r_y[0] + r_y[1] + r_y[2]
    to_z = pltpu.make_async_remote_copy(
        src_ref=s_y.at[1 - zhi], dst_ref=r_z, send_sem=z_send, recv_sem=z_recv,
        device_id=(other_z, g), device_id_type=MESH,
    )
    to_z.start()

    def drain(d, carry):
        @pl.when(jnp.logical_or(d > PLANES, sends_right))
        def _():
            halo_right(d).wait_send()

        @pl.when(jnp.logical_or(d > PLANES, sends_left))
        def _():
            halo_left(d).wait_send()

        return carry

    lax.fori_loop(1, reach + 1, drain, 0)
    for r in (1, 2, 3):
        field_right(r).wait_send()
        field_left(r).wait_send()

    @pl.when(k <= 13)
    def _():
        for p in order:
            move(p, lax.rem(k + 2, 16), mv_send.at[p], mv_recv.at[p]).wait_send()
        kinds(2).wait_send()

    @pl.when(k <= 14)
    def _():
        kinds(1).wait_send()

    @pl.when(k == 0)
    def _():
        for p in order:
            move(p, 1, mv_extra.at[p], mv_recv.at[p]).wait_send()

    @pl.when(relays)
    def _():
        from_relay().wait_send()

    @pl.when(skips_right)
    def _():
        for p in range(PLANES):
            skip_right(p).wait_send()

    @pl.when(skips_left)
    def _():
        for p in range(PLANES):
            skip_left(p).wait_send()

    to_core.wait_send()
    for dy in (1, 2, 3):
        to_y(dy).wait_send()
    to_z.wait()
    den[...] = (s_y[zhi] + r_z[...]) / contour


def per_device(
    incoming, backward, fields, block_types,
    axial_taps, lateral_taps, depth_taps, bend_diagonal, bend_coupling,
):
    n_gx = lax.axis_size("gx")
    contour = float(lax.axis_size("sec") * block_types.shape[1])
    vmem = pl.BlockSpec(memory_space=pltpu.VMEM)
    hbm = pl.BlockSpec(memory_space=pltpu.HBM)
    dma = pltpu.SemaphoreType.DMA
    f32 = jnp.float32
    hand, den = pl.pallas_call(
        functools.partial(body, n_gx, contour),
        out_shape=(
            jax.ShapeDtypeStruct((PLANES, ORIENT, CELLS), f32),
            jax.ShapeDtypeStruct((PLANES, 4, CELLS), f32),
        ),
        in_specs=[hbm] * 9,
        out_specs=(vmem, vmem),
        scratch_shapes=[
            pltpu.VMEM((PLANES, ORIENT, CELLS), f32),
            pltpu.VMEM((1, 4), jnp.int32),
            pltpu.VMEM((3, ORIENT), f32),
            pltpu.VMEM((3, ORIENT), f32),
            pltpu.VMEM((3, ORIENT), f32),
            pltpu.VMEM((1, ORIENT), f32),
            pltpu.VMEM((ORIENT, ORIENT), f32),
            pltpu.VMEM((SPAN, ORIENT, CELLS), f32),
            pltpu.VMEM(((LEVELS + 1) * SLOTS, CELLS, 128), f32),
            pltpu.VMEM((4, 80, 128), f32),
            pltpu.VMEM((7, 3, PLANES, CELLS), f32),
            pltpu.VMEM((SLOTS, CELLS, 128), jnp.bfloat16),
            pltpu.VMEM((3, 1, 4), jnp.int32),
            pltpu.VMEM((LEVELS, 128, 128), jnp.bfloat16),
            pltpu.VMEM((CELLS, 128), f32),
            pltpu.VMEM((CELLS, 128), f32),
            pltpu.VMEM((4, PLANES, ORIENT, CELLS), jnp.bfloat16),
            pltpu.VMEM((4, 2, CELLS, 128), f32),
            pltpu.VMEM((256, 256), jnp.bfloat16),
            pltpu.VMEM((8, 128), f32),
            pltpu.VMEM((2, 4, 2, PLANES, 4, CELLS), f32),
            pltpu.VMEM((4, 2, PLANES, 4, CELLS), f32),
            pltpu.VMEM((ORIENT, CELLS), f32),
            pltpu.VMEM((4, 2, PLANES, 4, CELLS), f32),
            pltpu.VMEM((3, 2, PLANES, 4, CELLS), f32),
            pltpu.VMEM((2, PLANES, 4, CELLS), f32),
            pltpu.VMEM((PLANES, 4, CELLS), f32),
            dma((4,)), dma((4,)), dma((4,)), dma((2,)), dma((4,)),
            dma((2, LEVELS)), dma((2, LEVELS)),
            dma((2, 3)), dma((2, 3)),
            dma((2,)), dma((2,)),
            dma((9,)),
            dma(()), dma(()),
            dma((3,)), dma((3,)),
            dma(()), dma(()),
        ],
        compiler_params=pltpu.CompilerParams(
            collective_id=0, has_side_effects=True, vmem_limit_bytes=67043328
        ),
        name="chain",
    )(
        incoming, backward, fields, block_types,
        axial_taps, lateral_taps, depth_taps, bend_diagonal[None], bend_coupling,
    )
    return hand[None], den


def solution(mesh):
    in_specs = (
        P("sec", "gx", None, None),
        P("sec", "gx", None, None),
        P(None, "gx", None),
        P("sec", None),
        P(), P(), P(), P(), P(),
    )
    out_specs = (P("sec", "gx", None, None), P("gx", "sec", None))
    return jax.shard_map(
        per_device, mesh=mesh, in_specs=in_specs, out_specs=out_specs, check_vma=False
    )
```
